32 devices in a mesh: scan: 4 (over y, x), slab: 8 (over z, core).
Axes of the slice: x: 2, y: 2, z: 4, core: 2. Of those that a mesh axis runs over, the one named last changes fastest.
Arguments:
- solution: float32 [1536, 2048], P(('scan', 'slab')), parts along dimension 0, may hold values from -6 to 6
- direction: float32 [1536, 2048], P(('scan', 'slab')), parts along dimension 0, may hold values from -20 to 20
- gradient: float32 [1536, 2048], P(('scan', 'slab')), parts along dimension 0, may hold values from -40 to 40
- residual: float32 [512, 64, 896], P(('scan', 'slab')), parts along dimension 0, may hold values from -20 to 20
- tiles: bfloat16 [4, 2048, 896], replicated, may hold values from -0.125 to 0.125
- offsets: int32 [512], P(('scan', 'slab')), parts along dimension 0, may hold values from 1 to 320, as said below
Outputs:
- solution_next: float32 [1536, 2048], P(('scan', 'slab')), parts along dimension 0
- residual_next: float32 [512, 64, 896], P(('scan', 'slab')), parts along dimension 0
- gradient_next: float32 [1536, 2048], P(('scan', 'slab')), parts along dimension 0
- direction_next: float32 [1536, 2048], P(('scan', 'slab')), parts along dimension 0
The draws below stay inside these ranges and needn't reach their ends.
There are 4 independent parts, one for each index of `scan`. The reference program is written for one: setup_inputs(seed, part) draws one part's arguments, and reference() takes and returns one part's arrays. A program takes and returns all parts, laid end to end along the dimension named above; an argument that names none is the same for every part. Nothing has to cross between parts.
Inputs may be any that keep to these rules, and one draw needn't show every extreme that they name: View v belongs to slab v // 16, whose planes are s * 48 to s * 48 + 47 for slab s; its window offsets[v] to offsets[v] + 63 meets that slab and lies within the slab before it, the slab itself and the slab after it; offsets are 1 or more.
All inputs are finite; a program needn't handle non-finite values.
Results may differ from the reference program's by a relative error of at most 0.0029.
Values may be sent and summed in bfloat16 or wider, within the bound.
A program may use at most 192 MiB of HBM per device.

```python
import math
import jax
import jax.numpy as jnp
from jax import lax

ZD = 48
DR = 64
DC = 896
P_SIZE = 2048
VIEW_DEV = 16
ANGLES = 4
NZ = 384
VIEWS = 128


def rising_draw(key, length, inner_dims):
    positions = jnp.arange(length, dtype=jnp.float32) / max(length - 1, 1)
    rising_scale = jnp.exp(positions * math.log(3.0)).reshape((length,) + (1,) * len(inner_dims))
    values = jnp.clip(jax.random.normal(key, (length,) + inner_dims, jnp.float32), -4.0, 4.0)
    return values * rising_scale


def draw_direction(key, part):
    return rising_draw(jax.random.fold_in(key, 11), NZ, (P_SIZE,))


def draw_gradient(key, part):
    overall = jnp.exp(jax.random.uniform(jax.random.fold_in(key, 21), (), jnp.float32, math.log(0.5), math.log(2.0)))
    return rising_draw(jax.random.fold_in(key, 12), NZ, (P_SIZE,)) * overall


def draw_residual(key, part):
    return rising_draw(jax.random.fold_in(key, 13), VIEWS, (DR, DC))


def draw_offsets(key, part):
    owners = jnp.arange(VIEWS, dtype=jnp.int32) // VIEW_DEV
    lowest = jnp.maximum(jnp.maximum((owners - 1) * ZD, owners * ZD - DR + 1), 1)
    highest = jnp.minimum(jnp.minimum(owners * ZD + ZD - 1, (owners + 2) * ZD - DR), NZ - DR)
    return jax.random.randint(jax.random.fold_in(key, 14), (VIEWS,), lowest, highest + 1, jnp.int32)


def block_levels(rng, extent, cuts, smallest, high):
    gain, own = 1.0, jax.random.fold_in(rng, 6)
    for dim, shards_of in cuts:
        steps = jnp.exp(jax.random.uniform(jax.random.fold_in(own, dim), (shards_of,), jnp.float32, smallest / len(cuts), high / len(cuts)))
        gain = gain * jnp.repeat(steps, extent[dim] // shards_of).reshape([-1 if axis == dim else 1 for axis in range(len(extent))])
    return gain


def scatter_about(own_key, dims, width, most, shards=(), held_as=jnp.bfloat16):
    drawn = width * jax.random.normal(own_key, dims, jnp.float32)
    if shards:
        drawn = drawn * block_levels(own_key, dims, shards, -0.22, 0.18)
    return jnp.clip(drawn, -most, most).astype(held_as)


def setup_inputs(seed: int = 0, part: int = 0) -> dict:
    arg_keys = jax.random.split(jax.random.key(seed), 7)
    part_keys = jax.random.split(jax.random.fold_in(arg_keys[6], part), 7)
    solution = scatter_about(part_keys[0], (NZ, P_SIZE), 1.0, 6.0, ((0, 8),), jnp.float32)
    direction = draw_direction(jax.random.fold_in(jax.random.fold_in(arg_keys[6], part), 71), part)
    gradient = draw_gradient(jax.random.fold_in(jax.random.fold_in(arg_keys[6], part), 71), part)
    residual = draw_residual(jax.random.fold_in(jax.random.fold_in(arg_keys[6], part), 71), part)
    tiles = scatter_about(arg_keys[4], (ANGLES, P_SIZE, DC), P_SIZE ** -0.5, 0.125)
    offsets = draw_offsets(jax.random.fold_in(jax.random.fold_in(arg_keys[6], part), 71), part)
    return dict(solution=solution, direction=direction, gradient=gradient, residual=residual, tiles=tiles, offsets=offsets)


def reference(solution, direction, gradient, residual, tiles, offsets):
    direction_half = direction.astype(jnp.bfloat16)
    view_total = offsets.shape[0]
    angle_ids = (jnp.arange(view_total, dtype=jnp.int32) % ANGLES).astype(jnp.int32)

    def forward_view(carried, view_item):
        first_row, angle_index = view_item
        window_rows = lax.dynamic_slice_in_dim(direction_half, first_row.astype(jnp.int32), DR, 0)
        angle_tile = lax.dynamic_index_in_dim(tiles, angle_index, 0, keepdims=False)
        return carried, jnp.dot(window_rows, angle_tile, preferred_element_type=jnp.float32)

    _, projected = lax.scan(forward_view, jnp.float32(0.0), (offsets, angle_ids))
    grad_norm = jnp.sum(gradient * gradient)
    image_norm = jnp.sum(projected * projected)
    step_size = grad_norm / image_norm
    solution_next = solution + step_size * direction
    residual_next = residual - step_size * projected
    residual_half = residual_next.astype(jnp.bfloat16)

    def backward_view(accumulated, view_item):
        first_row, angle_index, residual_rows = view_item
        angle_tile = lax.dynamic_index_in_dim(tiles, angle_index, 0, keepdims=False)
        contribution = lax.dot_general(residual_rows, angle_tile, (((1,), (1,)), ((), ())), preferred_element_type=jnp.float32)
        first_row = first_row.astype(jnp.int32)
        current = lax.dynamic_slice_in_dim(accumulated, first_row, DR, 0)
        return lax.dynamic_update_slice_in_dim(accumulated, current + contribution, first_row, 0), None

    empty = jnp.zeros((NZ, P_SIZE), jnp.float32)
    gradient_next, _ = lax.scan(backward_view, empty, (offsets, angle_ids, residual_half))
    new_norm = jnp.sum(gradient_next * gradient_next)
    direction_next = gradient_next + (new_norm / grad_norm) * direction
    return solution_next, residual_next, gradient_next, direction_next
```

```python
import functools

import jax
import jax.numpy as jnp
from jax import lax
from jax.experimental import pallas as pl
from jax.experimental.pallas import tpu as pltpu
from jax.sharding import PartitionSpec as P

CHUNK = 256
LANES = 128
VMEM_MIB = 38


def fold_lanes(row):
    total = row[:, :LANES]
    for start in range(LANES, row.shape[1], LANES):
        total = total + row[:, start : start + LANES]
    return total


def kernel(
    count,
    offsets_ref,
    direction_hbm,
    gradient_hbm,
    residual_hbm,
    tiles_hbm,
    residual_out,
    gradient_out,
    stats_out,
    direction_vm,
    gradient_vm,
    residual_vm,
    tiles_vm,
    nearby,
    projected,
    windows,
    hits,
    picks,
    half,
    summed,
    center,
    outgoing,
    incoming,
    stat_send,
    stat_recv,
    stats_vm,
    local_sems,
    tile_sems,
    halo_send,
    halo_recv,
    stat_send_sems,
    stat_recv_sems,
    back_send,
    back_recv,
):
    me = lax.axis_index("slab")
    planes, cells = direction_vm.shape
    views, rows, columns = residual_vm.shape
    angles = tiles_vm.shape[0]
    per_angle = views // angles
    near = 3 * planes
    chunks = cells // CHUNK
    has_low = me > 0
    has_high = me < count - 1

    load_direction = pltpu.make_async_copy(direction_hbm, direction_vm, local_sems.at[0])
    load_gradient = pltpu.make_async_copy(gradient_hbm, gradient_vm, local_sems.at[1])
    load_residual = pltpu.make_async_copy(residual_hbm, residual_vm, local_sems.at[2])

    def load_tile(a):
        return pltpu.make_async_copy(tiles_hbm.at[a], tiles_vm.at[a], tile_sems.at[a])

    load_direction.start()
    for a in range(angles):
        load_tile(a).start()
    load_gradient.start()
    load_residual.start()

    barrier = pltpu.get_barrier_semaphore()
    for d in range(1, count):
        pl.semaphore_signal(barrier, inc=1, device_id={"slab": lax.rem(me + d, count)})

    load_direction.wait()
    nearby[planes : 2 * planes, :] = direction_vm[...].astype(jnp.bfloat16)

    pad = jnp.zeros((planes, cells), jnp.bfloat16)

    @pl.when(jnp.logical_not(has_low))
    def _():
        nearby[:planes, :] = pad
        incoming[:, 1] = jnp.zeros((chunks, planes, CHUNK), jnp.float32)

    @pl.when(jnp.logical_not(has_high))
    def _():
        nearby[2 * planes :, :] = pad
        incoming[:, 0] = jnp.zeros((chunks, planes, CHUNK), jnp.float32)

    pl.semaphore_wait(barrier, count - 1)

    own = nearby.at[pl.ds(planes, planes)]
    to_low = pltpu.make_async_remote_copy(
        own, nearby.at[pl.ds(2 * planes, planes)], halo_send.at[0], halo_recv.at[0],
        device_id={"slab": lax.rem(me + count - 1, count)},
    )
    to_high = pltpu.make_async_remote_copy(
        own, nearby.at[pl.ds(0, planes)], halo_send.at[1], halo_recv.at[1],
        device_id={"slab": lax.rem(me + 1, count)},
    )

    @pl.when(has_low)
    def _():
        to_low.start()

    @pl.when(has_high)
    def _():
        to_high.start()

    plane_id = lax.broadcasted_iota(jnp.int32, (near, per_angle * rows), 0)
    row_id = lax.broadcasted_iota(jnp.int32, (near, per_angle * rows), 1)
    row_of = lax.broadcasted_iota(jnp.int32, (per_angle * rows, near), 0)
    plane_of = lax.broadcasted_iota(jnp.int32, (per_angle * rows, near), 1)
    shift = planes - me * planes
    for a in range(angles):
        base = jnp.zeros_like(row_id)
        for j in range(per_angle):
            first = offsets_ref[j * angles + a] + shift
            base = jnp.where(row_id >= j * rows, first - j * rows, base)
        hits[a] = jnp.where(plane_id == row_id + base, 1.0, 0.0).astype(jnp.bfloat16)
        base = jnp.zeros_like(row_of)
        for j in range(per_angle):
            first = offsets_ref[j * angles + a] + shift
            base = jnp.where(row_of >= j * rows, first - j * rows, base)
        picks[a] = jnp.where(plane_of == row_of + base, 1.0, 0.0).astype(jnp.bfloat16)

    @pl.when(has_low)
    def _():
        to_low.wait_send()
        to_high_recv = to_high
        to_high_recv.wait_recv()

    @pl.when(has_high)
    def _():
        to_high.wait_send()
        to_low.wait_recv()

    def forward(a, total):
        load_tile(a).wait()
        image = jnp.dot(nearby[...], tiles_vm[a], preferred_element_type=jnp.float32)
        upper = image.astype(jnp.bfloat16)
        projected[a, 0] = upper
        projected[a, 1] = (image - upper.astype(jnp.float32)).astype(jnp.bfloat16)
        covering = jnp.sum(hits[a].astype(jnp.float32), axis=1, keepdims=True)
        return total + jnp.sum(image * image * covering, axis=0, keepdims=True)

    image_part = lax.fori_loop(0, angles, forward, jnp.zeros((1, columns), jnp.float32))
    load_gradient.wait()
    grad_part = jnp.sum(gradient_vm[...] * gradient_vm[...], axis=0, keepdims=True)

    def exchange(index):
        copies = []
        for d in range(1, count):
            copies.append(
                pltpu.make_async_remote_copy(
                    stat_send.at[index], stat_recv.at[index, d],
                    stat_send_sems.at[index, d], stat_recv_sems.at[index, d],
                    device_id={"slab": lax.rem(me + d, count)},
                )
            )
        for copy in copies:
            copy.start()
        return copies

    def gather(index, copies):
        total = stat_send[index]
        for d, copy in enumerate(copies):
            copy.wait()
            total = total + stat_recv[index, d + 1]
        return total

    stat_send[0] = jnp.concatenate(
        [fold_lanes(grad_part), fold_lanes(image_part), jnp.zeros((6, LANES), jnp.float32)], axis=0
    )
    copies = exchange(0)

    def pick(a, carry):
        windows[a] = jnp.dot(picks[a], projected[a, 0], preferred_element_type=jnp.float32) + jnp.dot(
            picks[a], projected[a, 1], preferred_element_type=jnp.float32
        )
        return carry

    lax.fori_loop(0, angles, pick, 0)
    load_residual.wait()
    norms = gather(0, copies)
    grad_norm = jnp.sum(norms[0:1], axis=1, keepdims=True)
    image_norm = jnp.sum(norms[1:2], axis=1, keepdims=True)
    step_size = grad_norm / image_norm

    def update(v, carry):
        a = lax.rem(v, angles)
        j = lax.div(v, angles)
        image = windows[a, pl.ds(pl.multiple_of(j * rows, rows), rows), :]
        residual_next = residual_vm[v] - step_size * image
        residual_vm[v] = residual_next
        half[a, pl.ds(pl.multiple_of(j * rows, rows), rows), :] = residual_next.astype(jnp.bfloat16)
        return carry

    lax.fori_loop(0, views, update, 0)
    store_residual = pltpu.make_async_copy(residual_vm, residual_out, local_sems.at[3])
    store_residual.start()

    def gather_rows(a, carry):
        summed[a] = jnp.dot(hits[a], half[a], preferred_element_type=jnp.float32).astype(jnp.bfloat16)
        return carry

    lax.fori_loop(0, angles, gather_rows, 0)

    def back_copy(side, j):
        target = lax.rem(me + (count - 1 if side == 0 else 1), count)
        return pltpu.make_async_remote_copy(
            outgoing.at[j, side], incoming.at[j, side], back_send.at[side, j], back_recv.at[side, j],
            device_id={"slab": target},
        )

    def backward(j, carry):
        cut = pl.ds(pl.multiple_of(j * CHUNK, CHUNK), CHUNK)
        total = jnp.zeros((near, CHUNK), jnp.float32)
        for a in range(angles):
            total = total + lax.dot_general(
                summed[a], tiles_vm[a, cut, :], (((1,), (1,)), ((), ())),
                preferred_element_type=jnp.float32,
            )
        outgoing[j, 0] = total[:planes]
        outgoing[j, 1] = total[2 * planes :]
        center[j] = total[planes : 2 * planes]

        @pl.when(has_low)
        def _():
            back_copy(0, j).start()

        @pl.when(has_high)
        def _():
            back_copy(1, j).start()

        return carry

    lax.fori_loop(0, chunks, backward, 0)

    def combine(j, total):
        @pl.when(has_low)
        def _():
            back_copy(0, j).wait_send()
            back_copy(1, j).wait_recv()

        @pl.when(has_high)
        def _():
            back_copy(1, j).wait_send()
            back_copy(0, j).wait_recv()

        new = center[j] + incoming[j, 0] + incoming[j, 1]
        gradient_vm[:, pl.ds(pl.multiple_of(j * CHUNK, CHUNK), CHUNK)] = new
        return total + jnp.sum(new * new, axis=0, keepdims=True)

    new_part = lax.fori_loop(0, chunks, combine, jnp.zeros((1, CHUNK), jnp.float32))
    stat_send[1] = jnp.concatenate([fold_lanes(new_part), jnp.zeros((7, LANES), jnp.float32)], axis=0)
    copies = exchange(1)
    store_gradient = pltpu.make_async_copy(gradient_vm, gradient_out, local_sems.at[4])
    store_gradient.start()
    new_norm = jnp.sum(gather(1, copies)[0:1], axis=1, keepdims=True)
    stats_vm[...] = jnp.concatenate(
        [
            jnp.broadcast_to(step_size, (1, LANES)),
            jnp.broadcast_to(new_norm / grad_norm, (1, LANES)),
            jnp.zeros((6, LANES), jnp.float32),
        ],
        axis=0,
    )
    store_stats = pltpu.make_async_copy(stats_vm, stats_out, local_sems.at[5])
    store_stats.start()
    store_residual.wait()
    store_gradient.wait()
    store_stats.wait()


def finish(
    stats, solution_ref, direction_ref, gradient_ref, residual_ref,
    solution_out, residual_out, gradient_out, direction_out,
    solution_vm, direction_vm, gradient_vm, sems, residual_vm, residual_in, residual_sems,
):
    pieces = residual_ref.shape[0] // residual_vm.shape[1]
    span = residual_vm.shape[1]

    def part_in(p):
        return pltpu.make_async_copy(
            residual_ref.at[pl.ds(p * span, span)], residual_vm.at[p], residual_in.at[p]
        )

    def part_out(p):
        return pltpu.make_async_copy(
            residual_vm.at[p], residual_out.at[pl.ds(p * span, span)], residual_sems.at[p]
        )

    loads = [
        pltpu.make_async_copy(gradient_ref, gradient_vm, sems.at[0]),
        pltpu.make_async_copy(direction_ref, direction_vm, sems.at[1]),
        pltpu.make_async_copy(solution_ref, solution_vm, sems.at[2]),
    ]
    for p in range(pieces):
        part_in(p).start()
    for load in loads:
        load.start()
    for p in range(pieces):
        part_in(p).wait()
        part_out(p).start()
    for load in loads:
        load.wait()
    stores = [
        pltpu.make_async_copy(gradient_vm, gradient_out, sems.at[3]),
        pltpu.make_async_copy(direction_vm, direction_out, sems.at[4]),
        pltpu.make_async_copy(solution_vm, solution_out, sems.at[5]),
    ]
    stores[0].start()
    solution_vm[...] = solution_vm[...] + stats[0:1, 0:1] * direction_vm[...]
    stores[2].start()
    direction_vm[...] = gradient_vm[...] + stats[1:2, 0:1] * direction_vm[...]
    stores[1].start()
    for store in stores:
        store.wait()
    for p in range(pieces):
        part_out(p).wait()


def local(count, solution, direction, gradient, residual, tiles, offsets):
    planes, cells = solution.shape
    views, rows, columns = residual.shape
    angles = tiles.shape[0]
    per_angle = views // angles
    near = 3 * planes
    chunks = cells // CHUNK
    f32, bf16 = jnp.float32, jnp.bfloat16
    anywhere = pl.BlockSpec(memory_space=pl.ANY)
    residual_next, gradient_next, stats = pl.pallas_call(
        functools.partial(kernel, count),
        name="cgls_step",
        out_shape=(
            jax.ShapeDtypeStruct(residual.shape, f32),
            jax.ShapeDtypeStruct(gradient.shape, f32),
            jax.ShapeDtypeStruct((8, LANES), f32),
        ),
        in_specs=[pl.BlockSpec(memory_space=pltpu.SMEM)] + [anywhere] * 4,
        out_specs=(anywhere,) * 3,
        scratch_shapes=[
            pltpu.VMEM((planes, cells), f32),
            pltpu.VMEM((planes, cells), f32),
            pltpu.VMEM((views, rows, columns), f32),
            pltpu.VMEM((angles, cells, columns), bf16),
            pltpu.VMEM((near, cells), bf16),
            pltpu.VMEM((angles, 2, near, columns), bf16),
            pltpu.VMEM((angles, per_angle * rows, columns), f32),
            pltpu.VMEM((angles, near, per_angle * rows), bf16),
            pltpu.VMEM((angles, per_angle * rows, near), bf16),
            pltpu.VMEM((angles, per_angle * rows, columns), bf16),
            pltpu.VMEM((angles, near, columns), bf16),
            pltpu.VMEM((chunks, planes, CHUNK), f32),
            pltpu.VMEM((chunks, 2, planes, CHUNK), f32),
            pltpu.VMEM((chunks, 2, planes, CHUNK), f32),
            pltpu.VMEM((2, 8, LANES), f32),
            pltpu.VMEM((2, count, 8, LANES), f32),
            pltpu.VMEM((8, LANES), f32),
            pltpu.SemaphoreType.DMA((6,)),
            pltpu.SemaphoreType.DMA((angles,)),
            pltpu.SemaphoreType.DMA((2,)),
            pltpu.SemaphoreType.DMA((2,)),
            pltpu.SemaphoreType.DMA((2, count)),
            pltpu.SemaphoreType.DMA((2, count)),
            pltpu.SemaphoreType.DMA((2, chunks)),
            pltpu.SemaphoreType.DMA((2, chunks)),
        ],
        compiler_params=pltpu.CompilerParams(
            collective_id=0, has_side_effects=True, vmem_limit_bytes=VMEM_MIB * 1024 * 1024
        ),
    )(offsets, direction, gradient, residual, tiles)
    pieces = angles
    volume = jax.ShapeDtypeStruct(solution.shape, f32)
    return pl.pallas_call(
        finish,
        name="finish",
        out_shape=(volume, jax.ShapeDtypeStruct(residual.shape, f32), volume, volume),
        in_specs=[pl.BlockSpec(memory_space=pltpu.VMEM)] + [anywhere] * 4,
        out_specs=(anywhere,) * 4,
        scratch_shapes=[
            pltpu.VMEM((planes, cells), f32),
            pltpu.VMEM((planes, cells), f32),
            pltpu.VMEM((planes, cells), f32),
            pltpu.SemaphoreType.DMA((6,)),
            pltpu.VMEM((pieces, views // pieces, rows, columns), f32),
            pltpu.SemaphoreType.DMA((pieces,)),
            pltpu.SemaphoreType.DMA((pieces,)),
        ],
        compiler_params=pltpu.CompilerParams(vmem_limit_bytes=16 * 1024 * 1024),
    )(stats, solution, direction, gradient_next, residual_next)


def solution(mesh):
    placed = (
        P(("scan", "slab"), None),
        P(("scan", "slab"), None),
        P(("scan", "slab"), None),
        P(("scan", "slab"), None, None),
        P(),
        P(("scan", "slab")),
    )
    return jax.shard_map(
        functools.partial(local, mesh.shape["slab"]),
        mesh=mesh,
        in_specs=placed,
        out_specs=(
            P(("scan", "slab"), None),
            P(("scan", "slab"), None, None),
            P(("scan", "slab"), None),
            P(("scan", "slab"), None),
        ),
        check_vma=False,
    )
```
